32 devices in a mesh: seq: 32 (over z, y, x, core).
Axes of the slice: x: 2, y: 2, z: 4, core: 2. Of those that a mesh axis runs over, the one named last changes fastest.
Arguments:
- tokens: bfloat16 [4096, 1024], P('seq'), may hold values from -96 to 96
- query_weight: bfloat16 [1024, 1024], replicated, may hold values from -1 to 1
- key_weight: bfloat16 [1024, 512], replicated, may hold values from -1 to 1
- value_matrix: bfloat16 [1024, 512], replicated, may hold values from -0.1875 to 0.1875
- out_weight: bfloat16 [1024, 1024], replicated, may hold values from -0.1875 to 0.1875
- out_cotangent: bfloat16 [4096, 1024], P('seq'), may hold values from -6 to 6
Outputs:
- attn_out: bfloat16 [4096, 1024], P('seq')
- tokens_grad: bfloat16 [4096, 1024], P('seq')
- query_weight_grad: float32 [1024, 1024], P('seq')
- key_weight_grad: float32 [1024, 512], P('seq')
- value_weight_grad: float32 [1024, 512], P('seq')
- out_weight_grad: float32 [1024, 1024], P(None, 'seq')
The draws below stay inside these ranges and needn't reach their ends.
All inputs are finite; a program needn't handle non-finite values.
Results may differ from the reference program's by a relative error of at most 0.015.
The reference program's roundings to bfloat16 on the way count: a program that leaves them out, or rounds other values in their place, can miss the bound.
Values may be sent and summed in bfloat16 or wider, within the bound.
A program may use at most 128 MiB of HBM per device.

```python
import jax
import jax.numpy as jnp
from jax import lax

MODEL_SIZE = 1024
QUERY_HEADS = 16
KEY_HEADS = 8
HEAD_SIZE = 64
PRIOR_SHARDS = 2
DEVICE_TOKENS = 128
QUERY_PER_KEY = 2
TOKEN_COUNT = 4096
N_SEQ = 32


def paired_projections(key):
    anchor_row = jax.random.fold_in(key, 4711)
    query_piece = jnp.clip(jax.random.normal(jax.random.fold_in(anchor_row, 1), (MODEL_SIZE, QUERY_HEADS * HEAD_SIZE), jnp.float32), -6.0, 6.0) / MODEL_SIZE ** 0.5
    key_piece = jnp.clip(jax.random.normal(jax.random.fold_in(anchor_row, 2), (MODEL_SIZE, KEY_HEADS * HEAD_SIZE), jnp.float32), -6.0, 6.0) / MODEL_SIZE ** 0.5
    return (query_piece, key_piece)


def draw_query_weight(key, part):
    return paired_projections(key)[0].astype(jnp.bfloat16)


def draw_key_weight(key, part):
    return paired_projections(key)[1].astype(jnp.bfloat16)


def draw_tokens(key, part):
    row_ids = jnp.arange(TOKEN_COUNT, dtype=jnp.int32)
    raw = jnp.clip(jax.random.normal(jax.random.fold_in(key, 11), (TOKEN_COUNT, MODEL_SIZE), jnp.float32), -6.0, 6.0)
    values_now = raw
    order = jax.random.permutation(jax.random.fold_in(key, 14), N_SEQ)
    block_width = MODEL_SIZE // N_SEQ
    chosen = order[row_ids // DEVICE_TOKENS]
    lifted = jnp.where(jnp.arange(MODEL_SIZE, dtype=jnp.int32)[None, :] // block_width == chosen[:, None], 4.0, 1.0)
    return jnp.clip(values_now * lifted, -96.0, 96.0).astype(jnp.bfloat16)


def spiked(entries, rng, source, target, blocks, factor):
    owner, partner = [(jnp.arange(entries.shape[axis_at]) // (entries.shape[axis_at] // blocks)).reshape([-1 if axis == axis_at else 1 for axis in range(entries.ndim)]) for axis_at in (source, target)]
    chosen = jax.random.permutation(rng, blocks)[partner]
    strong = (owner == chosen) | (owner == (partner + blocks // 2) % blocks)
    return jnp.where(strong, factor * entries, entries)


def level_of(stream_key, extent, shards, smallest, high):
    def one(position, parts):
        draws = jax.random.uniform(jax.random.fold_in(jax.random.fold_in(stream_key, 6), position), (parts,), jnp.float32, smallest / len(shards), high / len(shards))
        return jnp.repeat(jnp.exp(draws), extent[position] // parts).reshape((-1,) + (1,) * (len(extent) - position - 1))

    factor_of = one(*shards[0])
    for cut in shards[1:]:
        factor_of = factor_of * one(*cut)
    return factor_of


def centred(rng, dims, scale, most, cuts=(), held_as=jnp.bfloat16):
    loudness = level_of(rng, dims, cuts, -0.22, 0.18) if cuts else 1.0
    drawn = jax.random.normal(rng, dims, jnp.float32) * scale * loudness
    return jnp.minimum(jnp.maximum(drawn, -most), most).astype(held_as)


def gaussian_with(own_key, extent, deviation, most, cuts, heavy, kind=jnp.bfloat16):
    values = deviation * jax.random.normal(own_key, extent, jnp.float32)
    if cuts:
        values = values * level_of(own_key, extent, cuts, -0.22, 0.18)
    return jnp.clip(spiked(values, jax.random.fold_in(own_key, 3), *heavy), -most, most).astype(kind)


def setup_inputs(seed: int = 0) -> dict:
    splits = jax.random.split(jax.random.key(seed), 7)
    tokens = draw_tokens(jax.random.fold_in(splits[6], 71), 0)
    query_weight = draw_query_weight(jax.random.fold_in(splits[6], 71), 0)
    key_weight = draw_key_weight(jax.random.fold_in(splits[6], 71), 0)
    value_matrix = centred(splits[3], (MODEL_SIZE, KEY_HEADS * HEAD_SIZE), MODEL_SIZE ** -0.5, 0.1875)
    out_weight = centred(splits[4], (QUERY_HEADS * HEAD_SIZE, MODEL_SIZE), (QUERY_HEADS * HEAD_SIZE) ** -0.5, 0.1875)
    out_cotangent = gaussian_with(splits[5], (TOKEN_COUNT, MODEL_SIZE), 1.0, 6.0, ((0, 32),), (0, 1, 32, 2.75))
    return dict(tokens=tokens, query_weight=query_weight, key_weight=key_weight, value_matrix=value_matrix, out_weight=out_weight, out_cotangent=out_cotangent)


SCALE = 0.125
MASKED = -1e30


def permitted(shard_idx):
    query_pos = shard_idx * DEVICE_TOKENS + jnp.arange(DEVICE_TOKENS, dtype=jnp.int32)
    key_pos = (shard_idx - PRIOR_SHARDS) * DEVICE_TOKENS + jnp.arange((PRIOR_SHARDS + 1) * DEVICE_TOKENS, dtype=jnp.int32)
    return (key_pos[None, :] <= query_pos[:, None]) & (key_pos[None, :] >= 0)


def split_queries(weight_matrix):
    return jnp.transpose(weight_matrix.reshape(weight_matrix.shape[0], KEY_HEADS, QUERY_PER_KEY, HEAD_SIZE), (1, 0, 2, 3))


def split_keys(weight_matrix):
    return jnp.transpose(weight_matrix.reshape(weight_matrix.shape[0], KEY_HEADS, HEAD_SIZE), (1, 0, 2))


def join_queries(head_rows):
    return jnp.transpose(head_rows, (1, 0, 2, 3)).reshape(head_rows.shape[1], QUERY_HEADS * HEAD_SIZE)


def join_keys(head_rows):
    return jnp.transpose(head_rows, (1, 0, 2)).reshape(head_rows.shape[1], KEY_HEADS * HEAD_SIZE)


def head_scores(queries, key_head, allowed):
    scores = jnp.einsum("tgd,wd->tgw", queries.astype(jnp.float32), key_head.astype(jnp.float32)) * SCALE
    return jnp.where(allowed[:, None, :], scores, MASKED)


def head_forward(queries, key_head, value_head, allowed):
    scores = head_scores(queries, key_head, allowed)
    highest = jnp.max(scores, axis=-1, keepdims=True)
    summed_total = jnp.sum(jnp.exp(scores - highest), axis=-1, keepdims=True)
    logsum = highest + jnp.log(summed_total)
    probs = jnp.exp(scores - logsum).astype(jnp.bfloat16)
    attended = jnp.einsum("tgw,wd->tgd", probs.astype(jnp.float32), value_head.astype(jnp.float32)).astype(jnp.bfloat16)
    return attended, logsum[..., 0]


def head_backward(queries, key_head, value_head, logsum, d_attended, attended, allowed):
    scores = head_scores(queries, key_head, allowed)
    weights = jnp.exp(scores - logsum[..., None])
    probs = weights.astype(jnp.bfloat16)
    d_float = d_attended.astype(jnp.float32)
    spread = jnp.sum(d_float * attended.astype(jnp.float32), axis=-1)
    value_part = jnp.einsum("tgw,tgd->wd", probs.astype(jnp.float32), d_float)
    dprobs = jnp.einsum("tgd,wd->tgw", d_float, value_head.astype(jnp.float32))
    dscores = (weights * (dprobs - spread[..., None])).astype(jnp.bfloat16)
    ds_float = dscores.astype(jnp.float32)
    query_piece = jnp.einsum("tgw,wd->tgd", ds_float, key_head.astype(jnp.float32)) * SCALE
    key_piece = jnp.einsum("tgw,tgd->wd", ds_float, queries.astype(jnp.float32)) * SCALE
    return query_piece, key_piece, value_part


def fold_window(pieces):
    pieces = pieces.reshape(N_SEQ, PRIOR_SHARDS + 1, DEVICE_TOKENS, KEY_HEADS * HEAD_SIZE)
    tail_rows = jnp.zeros((PRIOR_SHARDS, PRIOR_SHARDS + 1, DEVICE_TOKENS, KEY_HEADS * HEAD_SIZE), pieces.dtype)
    padded = jnp.concatenate([pieces, tail_rows], axis=0)
    summed_total = padded[0:N_SEQ, PRIOR_SHARDS]
    for offset in range(1, PRIOR_SHARDS + 1):
        summed_total = summed_total + padded[offset:offset + N_SEQ, PRIOR_SHARDS - offset]
    return summed_total.reshape(TOKEN_COUNT, KEY_HEADS * HEAD_SIZE).astype(jnp.bfloat16)


def reference(tokens, query_weight, key_weight, value_matrix, out_weight, out_cotangent):
    window = (PRIOR_SHARDS + 1) * DEVICE_TOKENS
    queries = jnp.dot(tokens, query_weight, preferred_element_type=jnp.float32).astype(jnp.bfloat16)
    keys_all = jnp.dot(tokens, key_weight, preferred_element_type=jnp.float32).astype(jnp.bfloat16)
    values_all = jnp.dot(tokens, value_matrix, preferred_element_type=jnp.float32).astype(jnp.bfloat16)
    leading_padding = jnp.zeros((PRIOR_SHARDS * DEVICE_TOKENS, KEY_HEADS * HEAD_SIZE), jnp.bfloat16)
    keys_padded = jnp.concatenate([leading_padding, keys_all], axis=0)
    values_padded = jnp.concatenate([leading_padding, values_all], axis=0)
    shard_ids = jnp.arange(N_SEQ, dtype=jnp.int32)

    def blocks_of(shard_idx):
        start_row = (shard_idx * DEVICE_TOKENS).astype(jnp.int32)
        q_block = lax.dynamic_slice_in_dim(queries, start_row, DEVICE_TOKENS, 0)
        k_block = lax.dynamic_slice_in_dim(keys_padded, start_row, window, 0)
        v_block = lax.dynamic_slice_in_dim(values_padded, start_row, window, 0)
        return split_queries(q_block), split_keys(k_block), split_keys(v_block)

    def forward_shard(shard_idx):
        allowed = permitted(shard_idx)
        q_heads, k_heads, v_heads = blocks_of(shard_idx)
        att_heads, logsum = lax.map(lambda operands: head_forward(operands[0], operands[1], operands[2], allowed), (q_heads, k_heads, v_heads))
        return join_queries(att_heads), logsum

    attended_all, logsum_all = lax.map(forward_shard, shard_ids)
    attended_all = attended_all.reshape(TOKEN_COUNT, QUERY_HEADS * HEAD_SIZE)
    attn_out = jnp.dot(attended_all, out_weight, preferred_element_type=jnp.float32).astype(jnp.bfloat16)
    out_weight_grad = jnp.dot(attended_all.T, out_cotangent, preferred_element_type=jnp.float32)
    d_attended = jnp.dot(out_cotangent, out_weight.T, preferred_element_type=jnp.float32).astype(jnp.bfloat16)

    def backward_shard(operands):
        shard_idx, logsum = operands
        allowed = permitted(shard_idx)
        q_heads, k_heads, v_heads = blocks_of(shard_idx)
        start_row = (shard_idx * DEVICE_TOKENS).astype(jnp.int32)
        d_heads = split_queries(lax.dynamic_slice_in_dim(d_attended, start_row, DEVICE_TOKENS, 0))
        a_heads = split_queries(lax.dynamic_slice_in_dim(attended_all, start_row, DEVICE_TOKENS, 0))
        q_part, k_part, v_part = lax.map(lambda inner: head_backward(inner[0], inner[1], inner[2], inner[3], inner[4], inner[5], allowed), (q_heads, k_heads, v_heads, logsum, d_heads, a_heads))
        return join_queries(q_part), join_keys(k_part), join_keys(v_part)

    q_parts, k_parts, v_parts = lax.map(backward_shard, (shard_ids, logsum_all))
    query_grad = q_parts.reshape(TOKEN_COUNT, QUERY_HEADS * HEAD_SIZE).astype(jnp.bfloat16)
    key_grad = fold_window(k_parts)
    value_grad = fold_window(v_parts)
    query_weight_grad = jnp.dot(tokens.T, query_grad, preferred_element_type=jnp.float32)
    key_weight_grad = jnp.dot(tokens.T, key_grad, preferred_element_type=jnp.float32)
    value_weight_grad = jnp.dot(tokens.T, value_grad, preferred_element_type=jnp.float32)
    tokens_grad = (jnp.dot(query_grad, query_weight.T, preferred_element_type=jnp.float32)
                   + jnp.dot(key_grad, key_weight.T, preferred_element_type=jnp.float32)
                   + jnp.dot(value_grad, value_matrix.T, preferred_element_type=jnp.float32)).astype(jnp.bfloat16)
    return (attn_out, tokens_grad, query_weight_grad, key_weight_grad, value_weight_grad, out_weight_grad)
```

```python
import jax
import jax.numpy as jnp
from jax import lax
from jax.experimental import pallas as pl
from jax.experimental.pallas import tpu as pltpu
from jax.sharding import PartitionSpec as P

HEAD_SIZE = 64
SCALE = 0.125
MASKED = -1e30
BF16 = jnp.bfloat16
F32 = jnp.float32


def dot(left, right, dims):
    return lax.dot_general(left, right, (dims, ((), ())), preferred_element_type=F32)


NN = ((1,), (0,))
NT = ((1,), (1,))
TN = ((0,), (0,))


def passed_along(block, axis, distance):
    devices = range(lax.axis_size(axis))
    route = [(i - distance, i) for i in devices if i - distance in devices]
    return lax.ppermute(block, axis, route)


def attention_kernel(
    q_ref, own_ref, near_ref, far_ref, d_ref, att_ref, qg_ref, own_out, near_out, far_out
):
    rows = q_ref.shape[0]
    key_columns = own_ref.shape[1] // 2
    window = 3 * rows
    shard = lax.axis_index("seq")
    query_row = lax.broadcasted_iota(jnp.int32, (2 * rows, window), 0)
    query_row = jnp.where(query_row >= rows, query_row - rows, query_row)
    key_row = lax.broadcasted_iota(jnp.int32, (2 * rows, window), 1)
    allowed = (key_row <= query_row + 2 * rows) & (key_row >= (2 - shard) * rows)

    def both_heads(ref, g):
        tile = ref[:, g * 2 * HEAD_SIZE : (g + 1) * 2 * HEAD_SIZE]
        return jnp.concatenate([tile[:, :HEAD_SIZE], tile[:, HEAD_SIZE:]], axis=0)

    def side_by_side(stacked):
        return jnp.concatenate([stacked[:rows], stacked[rows:]], axis=1)

    def one_group(g, keys, values):
        queries = both_heads(q_ref, g)
        d_att = both_heads(d_ref, g)
        scores = jnp.where(allowed, dot(queries, keys, NT) * SCALE, MASKED)
        highest = jnp.max(scores, axis=-1, keepdims=True)
        raised = jnp.exp(scores - highest)
        weights = raised * (1.0 / jnp.sum(raised, axis=-1, keepdims=True))
        probs = weights.astype(BF16)
        attended = dot(probs, values, NN).astype(BF16)
        spread = jnp.sum(d_att.astype(F32) * attended.astype(F32), axis=-1, keepdims=True)
        dprobs = dot(d_att, values, NT)
        dscores = (weights * (dprobs - spread)).astype(BF16)
        q_grad = (dot(dscores, keys, NN) * SCALE).astype(BF16)
        tile = slice(g * 2 * HEAD_SIZE, (g + 1) * 2 * HEAD_SIZE)
        att_ref[:, tile] = side_by_side(attended)
        qg_ref[:, tile] = side_by_side(q_grad)
        return dot(dscores, queries, TN) * SCALE, dot(probs, d_att, TN)

    for pair in range(key_columns // (2 * HEAD_SIZE)):
        tile = slice(pair * 2 * HEAD_SIZE, (pair + 1) * 2 * HEAD_SIZE)
        value_tile = slice(key_columns + tile.start, key_columns + tile.stop)
        sides = (far_ref, near_ref, own_ref)
        keys = jnp.concatenate([ref[:, tile] for ref in sides], axis=0)
        values = jnp.concatenate([ref[:, value_tile] for ref in sides], axis=0)
        k_low, v_low = one_group(2 * pair, keys[:, :HEAD_SIZE], values[:, :HEAD_SIZE])
        k_high, v_high = one_group(2 * pair + 1, keys[:, HEAD_SIZE:], values[:, HEAD_SIZE:])
        for where, low, high in ((tile, k_low, k_high), (value_tile, v_low, v_high)):
            part = jnp.concatenate([low, high], axis=1)
            far_out[:, where] = part[:rows].astype(BF16)
            near_out[:, where] = part[rows : 2 * rows].astype(BF16)
            own_out[:, where] = part[2 * rows :]


def attention(queries, own, near, far, d_attended):
    shape = jax.ShapeDtypeStruct
    vmem = pl.BlockSpec(memory_space=pltpu.VMEM)
    return pl.pallas_call(
        attention_kernel,
        out_shape=(
            shape(queries.shape, BF16),
            shape(queries.shape, BF16),
            shape(own.shape, F32),
            shape(own.shape, BF16),
            shape(own.shape, BF16),
        ),
        in_specs=[vmem] * 5,
        out_specs=(vmem,) * 5,
        cost_estimate=pl.CostEstimate(
            flops=10**9, bytes_accessed=4 * 10**6, transcendentals=10**6
        ),
        name="attention",
    )(queries, own, near, far, d_attended)


def scattered_sum(partial, axis, order):
    n = lax.axis_size(axis)
    me = lax.axis_index(axis)
    left = list(reversed(range(n.bit_length() - 1)))
    held = partial.reshape((2,) * len(left) + (partial.shape[0] // n, partial.shape[1]))
    for bit in order:
        at = left.index(bit)
        left.pop(at)
        mine = (me >> bit) & 1
        sent = lax.dynamic_index_in_dim(held, 1 - mine, at, keepdims=False).astype(BF16)
        kept = lax.dynamic_index_in_dim(held, mine, at, keepdims=False)
        got = lax.ppermute(sent, axis, [(i, i ^ (1 << bit)) for i in range(n)])
        held = kept.astype(F32) + got.astype(F32)
    return held


def shards(tokens, query_weight, key_weight, value_matrix, out_weight, out_cotangent):
    keys = dot(tokens, key_weight, NN).astype(BF16)
    values = dot(tokens, value_matrix, NN).astype(BF16)
    own = jnp.concatenate([keys, values], axis=1)
    near = passed_along(own, "seq", 1)
    far = passed_along(own, "seq", 2)
    queries = dot(tokens, query_weight, NN).astype(BF16)
    d_attended = dot(out_cotangent, out_weight, NT).astype(BF16)
    attended, query_grad, own_part, near_part, far_part = attention(
        queries, own, near, far, d_attended
    )
    near_back = passed_along(near_part, "seq", -1)
    far_back = passed_along(far_part, "seq", -2)
    bits = lax.axis_size("seq").bit_length() - 1
    rest = list(range(1, bits))
    orders = ([0] + rest, [0] + rest[1:] + rest[:1], [0] + rest[2:] + rest[:2])
    out_rows = scattered_sum(dot(out_cotangent, attended, TN), "seq", orders[0])
    query_rows = scattered_sum(dot(tokens, query_grad, TN), "seq", orders[1])
    attn_out = dot(attended, out_weight, NN).astype(BF16)
    both_grad = (own_part + near_back.astype(F32) + far_back.astype(F32)).astype(BF16)
    both_rows = scattered_sum(dot(tokens, both_grad, TN), "seq", orders[2])
    width = key_weight.shape[1]
    tokens_grad = (
        dot(query_grad, query_weight, NT)
        + dot(both_grad[:, :width], key_weight, NT)
        + dot(both_grad[:, width:], value_matrix, NT)
    ).astype(BF16)
    return (
        attn_out,
        tokens_grad,
        query_rows,
        both_rows[:, :width],
        both_rows[:, width:],
        out_rows.T,
    )


def solution(mesh):
    in_specs = (P("seq", None), P(), P(), P(), P(), P("seq", None))
    out_specs = (
        P("seq", None),
        P("seq", None),
        P("seq", None),
        P("seq", None),
        P("seq", None),
        P(None, "seq"),
    )
    return jax.shard_map(shards, mesh=mesh, in_specs=in_specs, out_specs=out_specs, check_vma=False)
```

```python
import jax
import jax.numpy as jnp
from jax import lax
from jax.experimental import pallas as pl
from jax.experimental.pallas import tpu as pltpu
from jax.sharding import PartitionSpec as P

HEAD_SIZE = 64
SCALE = 0.125
MASKED = -1e30
BF16 = jnp.bfloat16
F32 = jnp.float32


def dot(left, right, dims):
    return lax.dot_general(left, right, (dims, ((), ())), preferred_element_type=F32)


NN = ((1,), (0,))
NT = ((1,), (1,))
TN = ((0,), (0,))


def passed_along(block, axis, distance):
    devices = range(lax.axis_size(axis))
    route = [(i - distance, i) for i in devices if i - distance in devices]
    return lax.ppermute(block, axis, route)


def attention_kernel(
    q_ref, own_ref, near_ref, far_ref, d_ref, att_ref, qg_ref, own_out, near_out, far_out
):
    rows = q_ref.shape[0]
    key_columns = own_ref.shape[1] // 2
    window = 3 * rows
    shard = lax.axis_index("seq")
    query_row = lax.broadcasted_iota(jnp.int32, (2 * rows, window), 0)
    query_row = jnp.where(query_row >= rows, query_row - rows, query_row)
    key_row = lax.broadcasted_iota(jnp.int32, (2 * rows, window), 1)
    allowed = (key_row <= query_row + 2 * rows) & (key_row >= (2 - shard) * rows)

    def both_heads(ref, g):
        tile = ref[:, g * 2 * HEAD_SIZE : (g + 1) * 2 * HEAD_SIZE]
        return jnp.concatenate([tile[:, :HEAD_SIZE], tile[:, HEAD_SIZE:]], axis=0)

    def side_by_side(stacked):
        return jnp.concatenate([stacked[:rows], stacked[rows:]], axis=1)

    def one_group(g, keys, values):
        queries = both_heads(q_ref, g)
        d_att = both_heads(d_ref, g)
        scores = jnp.where(allowed, dot(queries, keys, NT) * SCALE, MASKED)
        highest = jnp.max(scores, axis=-1, keepdims=True)
        raised = jnp.exp(scores - highest)
        weights = raised * (1.0 / jnp.sum(raised, axis=-1, keepdims=True))
        probs = weights.astype(BF16)
        attended = dot(probs, values, NN).astype(BF16)
        spread = jnp.sum(d_att.astype(F32) * attended.astype(F32), axis=-1, keepdims=True)
        dprobs = dot(d_att, values, NT)
        dscores = (weights * (dprobs - spread)).astype(BF16)
        q_grad = (dot(dscores, keys, NN) * SCALE).astype(BF16)
        tile = slice(g * 2 * HEAD_SIZE, (g + 1) * 2 * HEAD_SIZE)
        att_ref[:, tile] = side_by_side(attended)
        qg_ref[:, tile] = side_by_side(q_grad)
        return dot(dscores, queries, TN) * SCALE, dot(probs, d_att, TN)

    for pair in range(key_columns // (2 * HEAD_SIZE)):
        tile = slice(pair * 2 * HEAD_SIZE, (pair + 1) * 2 * HEAD_SIZE)
        value_tile = slice(key_columns + tile.start, key_columns + tile.stop)
        sides = (far_ref, near_ref, own_ref)
        keys = jnp.concatenate([ref[:, tile] for ref in sides], axis=0)
        values = jnp.concatenate([ref[:, value_tile] for ref in sides], axis=0)
        k_low, v_low = one_group(2 * pair, keys[:, :HEAD_SIZE], values[:, :HEAD_SIZE])
        k_high, v_high = one_group(2 * pair + 1, keys[:, HEAD_SIZE:], values[:, HEAD_SIZE:])
        for where, low, high in ((tile, k_low, k_high), (value_tile, v_low, v_high)):
            part = jnp.concatenate([low, high], axis=1)
            far_out[:, where] = part[:rows].astype(BF16)
            near_out[:, where] = part[rows : 2 * rows].astype(BF16)
            own_out[:, where] = part[2 * rows :]


def attention(queries, own, near, far, d_attended):
    shape = jax.ShapeDtypeStruct
    vmem = pl.BlockSpec(memory_space=pltpu.VMEM)
    return pl.pallas_call(
        attention_kernel,
        out_shape=(
            shape(queries.shape, BF16),
            shape(queries.shape, BF16),
            shape(own.shape, F32),
            shape(own.shape, BF16),
            shape(own.shape, BF16),
        ),
        in_specs=[vmem] * 5,
        out_specs=(vmem,) * 5,
        cost_estimate=pl.CostEstimate(
            flops=10**9, bytes_accessed=4 * 10**6, transcendentals=10**6
        ),
        name="attention",
    )(queries, own, near, far, d_attended)


def scattered_sum(partial, axis, order):
    n = lax.axis_size(axis)
    me = lax.axis_index(axis)
    left = list(reversed(range(n.bit_length() - 1)))
    held = partial.reshape((2,) * len(left) + (partial.shape[0] // n, partial.shape[1]))
    for bit in order:
        at = left.index(bit)
        left.pop(at)
        mine = (me >> bit) & 1
        sent = lax.dynamic_index_in_dim(held, 1 - mine, at, keepdims=False).astype(BF16)
        kept = lax.dynamic_index_in_dim(held, mine, at, keepdims=False)
        got = lax.ppermute(sent, axis, [(i, i ^ (1 << bit)) for i in range(n)])
        held = kept.astype(F32) + got.astype(F32)
    return held


def shards(tokens, query_weight, key_weight, value_matrix, out_weight, out_cotangent):
    keys = dot(tokens, key_weight, NN).astype(BF16)
    values = dot(tokens, value_matrix, NN).astype(BF16)
    own = jnp.concatenate([keys, values], axis=1)
    near = passed_along(own, "seq", 1)
    far = passed_along(own, "seq", 2)
    queries = dot(tokens, query_weight, NN).astype(BF16)
    d_attended = dot(out_cotangent, out_weight, NT).astype(BF16)
    attended, query_grad, own_part, near_part, far_part = attention(
        queries, own, near, far, d_attended
    )
    near_back = passed_along(near_part, "seq", -1)
    far_back = passed_along(far_part, "seq", -2)
    bits = lax.axis_size("seq").bit_length() - 1
    rest = list(range(1, bits))
    orders = ([0] + rest, [0] + rest[1::-1] + rest[2:], [0] + rest[2:] + rest[:2])
    out_rows = scattered_sum(dot(out_cotangent, attended, TN), "seq", orders[0])
    query_rows = scattered_sum(dot(tokens, query_grad, TN), "seq", orders[1])
    attn_out = dot(attended, out_weight, NN).astype(BF16)
    both_grad = (own_part + near_back.astype(F32) + far_back.astype(F32)).astype(BF16)
    both_rows = scattered_sum(dot(tokens, both_grad, TN), "seq", orders[2])
    width = key_weight.shape[1]
    tokens_grad = (
        dot(query_grad, query_weight, NT)
        + dot(both_grad[:, :width], key_weight, NT)
        + dot(both_grad[:, width:], value_matrix, NT)
    ).astype(BF16)
    return (
        attn_out,
        tokens_grad,
        query_rows,
        both_rows[:, :width],
        both_rows[:, width:],
        out_rows.T,
    )


def solution(mesh):
    in_specs = (P("seq", None), P(), P(), P(), P(), P("seq", None))
    out_specs = (
        P("seq", None),
        P("seq", None),
        P("seq", None),
        P("seq", None),
        P("seq", None),
        P(None, "seq"),
    )
    return jax.shard_map(shards, mesh=mesh, in_specs=in_specs, out_specs=out_specs, check_vma=False)
```
